128 devices in a mesh: sess: 32 (over x, z, core), tp: 4 (over y).
Axes of the slice: x: 4, y: 4, z: 4, core: 2. Of those that a mesh axis runs over, the one named last changes fastest.
Arguments:
- hidden: bfloat16 [16384, 8192], P('sess'), may hold values from -6 to 6
- routes: int32 [16384, 1], replicated, may hold values from 0 to 63; in each aligned block of 512 rows (0 to 511, 512 to 1023, ...) at most 16 rows name the same one
- w_qkv: bfloat16 [8192, 4, 1280], P(None, 'tp'), may hold values from -0.0625 to 0.0625
- b_qkv: float32 [4, 1280], P('tp'), may hold values from -8 to 8
- pool: bfloat16 [512, 4, 64, 256], P('sess', 'tp'), may hold values from -8 to 8
- page_lists: int32 [64, 4, 8], replicated, may hold values from 0 to 511, as said below
Outputs:
- attn_out: bfloat16 [64, 512, 4096], P('sess', None, 'tp')
The draws below stay inside these ranges and needn't reach their ends.
Inputs may be any that keep to these rules, and one draw needn't show every extreme that they name: `routes`: within the rows of one ingest index no session is named by more than 16 rows, a bound that some block reaches. `page_lists`: page p lies on pool index p // 16. For the sessions of one owner (sessions o * 2 to o * 2 + 1) and one 4 head, the 16 listed pages lie on distinct pool indices, exactly 1 on each of them.
All inputs are finite; a program needn't handle non-finite values.
Results may differ from the reference program's by a relative error of at most 0.0065.
Values may be sent and summed in bfloat16 or wider, within the bound.
A program may use at most 192 MiB of HBM per device.

```python
import math
import jax
import jax.numpy as jnp
import numpy as np
from jax import lax

D = 8192
HD = 128
QPK = 8
SESS_DEV = 2
ROWS_DEV = 512
KEPT = 8
PAGE = 64
POOL_DEV = 16
SESSIONS = 64
ROWS = 16384
ROW_MOST = 16
SEG = 512
PAGE_MOST = 1
POOL = 512
KV = 4
CW = 1280
N_SESS = 32


def draw_b_qkv(key, part):
    width = (QPK + 2) * HD
    noise = jax.random.normal(jax.random.fold_in(key, 21), (KV, width), jnp.float32)
    return jnp.clip(noise, -4.0, 4.0)


def draw_pool(key, part):
    shape = (POOL, KV, PAGE, 2 * HD)
    base = jax.random.normal(jax.random.fold_in(key, 31), shape, jnp.float32)
    return jnp.clip(base, -6.0, 6.0).astype(jnp.bfloat16)


def draw_page_lists(key, part):
    requests = SESS_DEV * KEPT
    grid_keys = jax.random.split(jax.random.fold_in(key, 41), N_SESS * KV)
    orders = jax.vmap(lambda single: jax.random.permutation(single, N_SESS))(grid_keys).reshape(N_SESS, KV, N_SESS)
    picks = jnp.arange(requests) // PAGE_MOST
    devices = orders[:, :, picks]
    slots = jax.random.randint(jax.random.fold_in(key, 42), (N_SESS, KV, requests), 0, POOL_DEV)
    pages = devices * POOL_DEV + slots
    pages = pages.reshape(N_SESS, KV, SESS_DEV, KEPT).transpose(0, 2, 1, 3).reshape(SESSIONS, KV, KEPT)
    return pages.astype(jnp.int32)


def block_levels(own_key, dims, cuts, low, high):
    def one(dim, parts):
        steps = jax.random.uniform(jax.random.fold_in(jax.random.fold_in(own_key, 6), dim), (parts,), jnp.float32, low / len(cuts), high / len(cuts))
        return jnp.repeat(jnp.exp(steps), dims[dim] // parts).reshape((-1,) + (1,) * (len(dims) - dim - 1))

    loudness = one(*cuts[0])
    for cut in cuts[1:]:
        loudness = loudness * one(*cut)
    return loudness


def assign_block(key, own, number, rows, number_of, top, limit, lean):
    order = jax.random.permutation(key, number_of)
    crowded, ordinary = shares(number_of, rows * top, limit, lean, True), shares(number_of, rows * top, limit, lean, False)
    places = jnp.arange(number_of)

    def named(lengths, offset_by):
        used = int((lengths > 0).sum())
        fixed = max(1, used // 4)
        moved = fixed + (places - fixed + offset_by * (used - fixed)) % max(1, number_of - fixed)
        return jnp.zeros((number_of,), jnp.int32).at[order[jnp.where(places < fixed, places, moved)]].set(jnp.asarray(lengths, jnp.int32))

    lengths = jnp.where(number % 4 == 0, named(crowded, number // 4), named(ordinary, number - number // 4 - 1))
    mixed = jax.random.permutation(jax.random.fold_in(own, 3), number_of)
    source_of, receiver = mixed[0:number_of // 2 * 2:2], mixed[1:number_of // 2 * 2:2]
    room = jnp.minimum(lengths[source_of] - 1, limit - lengths[receiver]) // 2
    room = jnp.where((source_of == order[0]) | (receiver == order[0]) | (lengths[receiver] == 0), 0, jnp.maximum(room, 0))
    moved = jax.random.randint(jax.random.fold_in(own, 4), (number_of // 2,), 0, 1 << 20) % (room + 1)
    lengths = lengths.at[source_of].add(-moved).at[receiver].add(moved)
    members = jnp.searchsorted(jnp.cumsum(lengths), jnp.arange(rows * top), side="right").astype(jnp.int32)
    table = members.reshape(top, rows).T
    table = table[jax.random.permutation(jax.random.fold_in(own, 1), rows)]
    offset_by = jax.random.randint(jax.random.fold_in(own, 2), (rows, 1), 0, top)
    return jnp.take_along_axis(table, (jnp.arange(top)[None, :] + offset_by) % top, axis=1)


def shares(amount, total, most, lean, full):
    loads = [(1 << 20) // math.isqrt(rank ** lean) + 1 for rank in range(1, amount + 1)]
    largest = most if full else min(most, max(-(-total // amount), total * loads[0] // sum(loads)))
    least = 1 if total - largest >= amount - 1 else 0
    given, spare = [largest] + [least] * (amount - 1), total - largest - least * (amount - 1)
    while spare > 0:
        free = [i for i in range(1, amount) if given[i] < largest] or [i for i in range(1, amount) if given[i] < most]
        whole, remaining = sum([loads[i] for i in free]), spare
        for i in free:
            more = min(most - given[i], max(1, remaining * loads[i] // whole), spare)
            given[i] = given[i] + more
            spare = spare - more
    return np.array(given)


def centred(key, extent, scale, limit, shards=(), kind=jnp.bfloat16):
    result = jax.random.normal(key, extent, jnp.float32) * scale
    if len(shards) > 0:
        result = block_levels(key, extent, shards, -0.22, 0.18) * result
    return jnp.clip(result, min=-limit, max=limit).astype(kind)


def setup_inputs(seed: int = 0) -> dict:
    splits = jax.random.split(jax.random.key(seed), 7)
    hidden = centred(splits[0], (ROWS, D), 1.0, 6.0, ((0, 32),))
    routes_keys = jax.random.split(jax.random.fold_in(splits[1], 1), ROWS // ROWS_DEV)
    routes_turns = jax.random.permutation(jax.random.fold_in(splits[1], 3), ROWS // ROWS_DEV)
    routes = jax.vmap(lambda own, number: assign_block(jax.random.fold_in(splits[1], 2), own, number, ROWS_DEV, SESSIONS, 1, ROW_MOST, 2))(routes_keys, routes_turns).reshape((ROWS, 1))
    w_qkv = centred(splits[2], (D, KV, CW), D ** -0.5, 0.0625, ((1, 4),))
    b_qkv = draw_b_qkv(jax.random.fold_in(splits[6], 71), 0)
    pool = draw_pool(jax.random.fold_in(splits[6], 71), 0)
    page_lists = draw_page_lists(jax.random.fold_in(splits[6], 71), 0)
    return {"hidden": hidden, "routes": routes, "w_qkv": w_qkv, "b_qkv": b_qkv, "pool": pool, "page_lists": page_lists}


def reference(hidden, routes, w_qkv, b_qkv, pool, page_lists):
    width = (QPK + 2) * HD
    scale = 1.0 / math.sqrt(HD)
    projected = jnp.dot(hidden, w_qkv.reshape(D, KV * width), preferred_element_type=jnp.float32)
    projected = (projected + b_qkv.reshape(1, KV * width)).astype(jnp.bfloat16).reshape(ROWS, KV, width)
    blocks = routes[:, 0].reshape(N_SESS, ROWS_DEV)
    session_ids = jnp.arange(SESSIONS, dtype=jnp.int32)
    onehot = (blocks[:, :, None] == session_ids[None, None, :]).astype(jnp.int32)
    ranking = lax.optimization_barrier(jnp.sum(jnp.cumsum(onehot, axis=1) * onehot, axis=2)) - 1
    counts = lax.optimization_barrier(jnp.sum(onehot, axis=1)).T
    slot_index = (jnp.arange(N_SESS, dtype=jnp.int32)[:, None] * ROW_MOST + ranking).reshape(ROWS)
    turn = jnp.zeros((SESSIONS, SEG, KV, width), jnp.bfloat16)
    turn = turn.at[blocks.reshape(ROWS), slot_index].set(projected)
    starts = jnp.cumsum(counts, axis=1) - counts
    offsets = jnp.arange(ROW_MOST, dtype=jnp.int32)
    live = (offsets[None, None, :] < counts[:, :, None]).reshape(SESSIONS, SEG)
    position = (starts[:, :, None] + offsets[None, None, :]).reshape(SESSIONS, SEG)
    heads = jnp.arange(KV, dtype=jnp.int32)
    history = pool[page_lists, heads[None, :, None]].reshape(SESSIONS, KV, KEPT * PAGE, 2 * HD)
    query_cols = QPK * HD

    def attend(items):
        rows, past, alive, placed = items
        query = rows[:, :, :query_cols].reshape(SEG, KV, QPK, HD).astype(jnp.float32)
        new_keys = jnp.transpose(rows[:, :, query_cols:query_cols + HD], (1, 0, 2))
        new_values = jnp.transpose(rows[:, :, query_cols + HD:], (1, 0, 2))
        keys = jnp.concatenate([past[:, :, :HD], new_keys], axis=1).astype(jnp.float32)
        values = jnp.concatenate([past[:, :, HD:], new_values], axis=1).astype(jnp.float32)
        scores = jnp.einsum('skgd,knd->kgsn', query, keys) * scale
        recent = alive[None, :] & (placed[None, :] <= placed[:, None])
        allowed = jnp.concatenate([jnp.ones((SEG, KEPT * PAGE), jnp.bool_), recent], axis=1)
        scores = jnp.where(allowed[None, None], scores, -1e+30)
        top = lax.optimization_barrier(jnp.max(scores, axis=-1, keepdims=True))
        expo = jnp.where(allowed[None, None], jnp.exp(scores - top), 0.0)
        probs = (expo / lax.optimization_barrier(jnp.sum(expo, axis=-1, keepdims=True))).astype(jnp.bfloat16)
        mixed = jnp.einsum('kgsn,knd->skgd', probs.astype(jnp.float32), values)
        mixed = jnp.where(alive[:, None, None, None], mixed, 0.0)
        return mixed.reshape(SEG, KV * QPK * HD).astype(jnp.bfloat16)
    return lax.map(attend, (turn, history, live, position))
```

```python
import functools
import math

import jax
import jax.numpy as jnp
from jax import lax
from jax.experimental import pallas as pl
from jax.experimental.pallas import tpu as pltpu
from jax.sharding import PartitionSpec as P

HD = 128
QPK = 8
UNIT = 128
CHUNK = 256
MESH = pl.DeviceIdType.MESH
NT = (((1,), (1,)), ((), ()))


def body(
    n, rows, depth, parts, kept, page, per_owner, slot_most, pool_dev,
    hidden_hbm, w_hbm, bias_ref, routes_ref, lists_ref, pool_hbm, out_hbm,
    hid, wv, biasv, acc, projv, place, send, recv, psend, precv, poolv,
    keys, vals, mask, alive, outv,
    hid_sem, w_sem, pool_sem, ps_sem, pr_sem, send_sem, recv_sem, out_sem,
):
    f32, bf16, i32 = jnp.float32, jnp.bfloat16, jnp.int32
    me = lax.axis_index("sess")
    head = lax.axis_index("tp")
    sessions = n * per_owner
    seg = n * slot_most
    hist = kept * page
    slots = sessions * slot_most
    chunks = (QPK + 2) * HD // CHUNK
    block = depth // parts

    barrier = pltpu.get_barrier_semaphore()

    def greet(k, carry):
        pl.semaphore_signal(
            barrier, inc=1, device_id={"sess": lax.rem(me + k, n)}, device_id_type=MESH
        )
        return carry

    lax.fori_loop(1, n, greet, 0)

    def pool_copy():
        return pltpu.make_async_copy(pool_hbm, poolv, pool_sem)

    def hid_copy(k):
        return pltpu.make_async_copy(
            hidden_hbm.at[:, pl.ds(k * block, block)], hid.at[k], hid_sem.at[k]
        )

    def w_copy(c, k):
        first = lax.rem(c + chunks - 1, chunks) * CHUNK
        return pltpu.make_async_copy(
            w_hbm.at[pl.ds(pl.multiple_of(k * block, block), block),
                     pl.ds(pl.multiple_of(first, CHUNK), CHUNK)],
            wv.at[c, k],
            w_sem.at[c, k],
        )

    pool_copy().start()
    for k in range(parts):
        hid_copy(k).start()
        w_copy(0, k).start()

    def fetch(i, carry):
        w_copy(1 + i // parts, i % parts).start()
        return carry

    lax.fori_loop(0, (chunks - 1) * parts, fetch, 0)

    pool_copy().wait()

    def pick(o, carry):
        chosen = jnp.int32(0)
        for l in range(per_owner):
            for k in range(kept):
                listed = lists_ref[head, k, o * per_owner + l]
                chosen = chosen + jnp.where(listed // pool_dev == me, listed % pool_dev, 0)
        psend[o] = poolv[chosen]
        return carry

    lax.fori_loop(0, n, pick, 0)
    precv[me] = psend[me]

    pl.semaphore_wait(barrier, n - 1)

    def page_copy(k):
        to = lax.rem(me + k, n)
        return pltpu.make_async_remote_copy(
            src_ref=psend.at[to], dst_ref=precv.at[me], send_sem=ps_sem, recv_sem=pr_sem,
            device_id={"sess": to}, device_id_type=MESH,
        )

    def send_page(k, carry):
        page_copy(k).start()
        return carry

    lax.fori_loop(1, n, send_page, 0)

    destination = routes_ref[pl.ds(me, 1), :]
    onehot = (lax.broadcasted_iota(i32, (sessions, rows), 0) == destination).astype(f32)
    earlier = (
        lax.broadcasted_iota(i32, (rows, rows), 0) < lax.broadcasted_iota(i32, (rows, rows), 1)
    ).astype(bf16)
    before = jnp.dot(onehot.astype(bf16), earlier, preferred_element_type=f32)
    ranking = jnp.sum(onehot * before, axis=0, keepdims=True)
    target = destination.astype(f32) * float(slot_most) + ranking
    steps = slots // CHUNK

    def fill(m, carry):
        ids = lax.broadcasted_iota(i32, (CHUNK, rows), 0) + m * CHUNK
        place[m] = (ids.astype(f32) == target).astype(bf16)
        return carry

    lax.fori_loop(0, steps, fill, 0)

    width = routes_ref.shape[0]
    for l in range(per_owner):
        same = (routes_ref[...] == me * per_owner + l).astype(f32)
        count_col = jnp.sum(same, axis=1, keepdims=True)
        count_row = lax.dot_general(
            jnp.ones((8, rows), bf16), same.astype(bf16), NT, preferred_element_type=f32
        )
        spread = (
            lax.broadcasted_iota(i32, (width, seg), 1) // slot_most
            == lax.broadcasted_iota(i32, (width, seg), 0)
        ).astype(bf16)
        spread_t = (
            lax.broadcasted_iota(i32, (seg, width), 0) // slot_most
            == lax.broadcasted_iota(i32, (seg, width), 1)
        ).astype(bf16)
        row_counts = jnp.dot(count_row.astype(bf16), spread, preferred_element_type=f32)
        col_counts = jnp.dot(
            spread_t, jnp.broadcast_to(count_col, (width, HD)).astype(bf16),
            preferred_element_type=f32,
        )
        row_off = (lax.broadcasted_iota(i32, (8, seg), 1) % slot_most).astype(f32)
        col_off = (lax.broadcasted_iota(i32, (seg, HD), 0) % slot_most).astype(f32)
        alive[l] = (col_off < col_counts).astype(f32)
        live_row = jnp.where(row_off < row_counts, 0.0, -1e30)[0:1, :]
        mask[l] = jnp.where(
            lax.broadcasted_iota(i32, (seg, seg), 1) <= lax.broadcasted_iota(i32, (seg, seg), 0),
            live_row, -1e30,
        )
        vals[l, :, HD:] = jnp.ones((hist + seg, HD), bf16)

    for c in range(chunks):
        first = ((c + chunks - 1) % chunks) * CHUNK
        biasv[c] = jnp.broadcast_to(bias_ref[0:1, first : first + CHUNK], (8, CHUNK))

    def row_copy(u, k):
        to = lax.rem(me + k, n)
        return pltpu.make_async_remote_copy(
            src_ref=send.at[u, pl.ds(to * per_owner, per_owner)],
            dst_ref=recv.at[u, :, pl.ds(pl.multiple_of(me * slot_most, slot_most), slot_most)],
            send_sem=send_sem.at[u], recv_sem=recv_sem.at[u],
            device_id={"sess": to}, device_id_type=MESH,
        )

    def project(c, carry):
        acc[...] = jnp.zeros_like(acc)

        def multiply(k, inner):
            @pl.when(c == 0)
            def _():
                hid_copy(k).wait()

            w_copy(c, k).wait()
            acc[...] += jnp.dot(hid[k], wv[c, k], preferred_element_type=f32)
            return inner

        lax.fori_loop(0, parts, multiply, 0)
        projv[...] = (acc[...] + biasv[c][0:1, :]).astype(bf16)

        def put(m, inner):
            placed = jnp.dot(place[m], projv[...], preferred_element_type=f32).astype(bf16)
            group = CHUNK // slot_most
            at = pl.ds(m * group, group)
            send[2 * c, at] = placed[:, :UNIT].reshape(group, slot_most, UNIT)
            send[2 * c + 1, at] = placed[:, UNIT:].reshape(group, slot_most, UNIT)
            return inner

        lax.fori_loop(0, steps, put, 0)

        def ship(k, inner):
            row_copy(2 * c, k).start()
            row_copy(2 * c + 1, k).start()
            return inner

        lax.fori_loop(1, n, ship, 0)
        own = pl.ds(pl.multiple_of(me * slot_most, slot_most), slot_most)
        for u in range(2):
            recv[2 * c + u, :, own, :] = send[2 * c + u, pl.ds(me * per_owner, per_owner)]
        return carry

    lax.fori_loop(0, chunks, project, 0)

    def arrived(u):
        part = recv.at[u, :, pl.ds(0, seg - slot_most)]
        pltpu.make_async_copy(part, part, recv_sem.at[u]).wait()

    part = precv.at[pl.ds(0, n - 1)]
    pltpu.make_async_copy(part, part, pr_sem).wait()
    for l in range(per_owner):
        for k in range(kept):
            source = lists_ref[head, k, me * per_owner + l] // pool_dev
            got = precv[source]
            keys[l, k * page : (k + 1) * page, :] = got[:, :HD]
            vals[l, k * page : (k + 1) * page, :HD] = got[:, HD:]
    arrived(0)
    arrived(1)
    for l in range(per_owner):
        keys[l, hist:, :] = recv[0, l]
        vals[l, hist:, :HD] = recv[1, l]

    tile = min(seg, 256)
    factor = math.log2(math.e) / math.sqrt(HD)

    def out_copy(h):
        return pltpu.make_async_copy(
            outv.at[h], out_hbm.at[:, :, pl.ds(pl.multiple_of(h * HD, HD), HD)], out_sem.at[h]
        )

    def attend(h, carry):
        arrived(2 + h)
        for l in range(per_owner):
            for start in range(0, seg, tile):
                upto = start + tile
                query = recv[2 + h, l, start:upto, :]
                past = lax.dot_general(query, keys[l, :hist, :], NT, preferred_element_type=f32)
                turn = lax.dot_general(
                    query, keys[l, hist : hist + upto, :], NT, preferred_element_type=f32
                )
                turn = turn + mask[l, start:upto, :upto]
                top = jnp.maximum(
                    jnp.max(past, axis=1, keepdims=True), jnp.max(turn, axis=1, keepdims=True)
                )
                past = jnp.exp2((past - top) * factor).astype(bf16)
                turn = jnp.exp2((turn - top) * factor).astype(bf16)
                total = jnp.dot(past, vals[l, :hist, :], preferred_element_type=f32)
                total += jnp.dot(turn, vals[l, hist : hist + upto, :], preferred_element_type=f32)
                mixed = total[:, :HD] / total[:, HD:]
                mixed = jnp.where(alive[l, start:upto, :] > 0.0, mixed, 0.0)
                outv[h, l, start:upto, :] = mixed.astype(bf16)
        out_copy(h).start()
        return carry

    lax.fori_loop(0, QPK, attend, 0)

    def finish(h, carry):
        out_copy(h).wait()
        return carry

    lax.fori_loop(0, QPK, finish, 0)
    part = psend.at[pl.ds(0, n - 1)]
    pltpu.make_async_copy(part, part, ps_sem).wait()

    def sent(u, carry):
        part = send.at[u, pl.ds(0, sessions - per_owner)]
        pltpu.make_async_copy(part, part, send_sem.at[u]).wait()
        return carry

    lax.fori_loop(0, 2 * chunks, sent, 0)


def on_device(hidden, routes, w_qkv, b_qkv, pool, page_lists):
    n = lax.axis_size("sess")
    rows, depth = hidden.shape
    sessions, _, kept = page_lists.shape
    per_owner = sessions // n
    slot_most = 2 * rows // sessions
    seg = n * slot_most
    pool_dev, _, page, pair = pool.shape
    hist = kept * page
    columns = (QPK + 2) * HD
    chunks = columns // CHUNK
    units = columns // UNIT
    parts = 8
    f32, bf16 = jnp.float32, jnp.bfloat16
    vmem, anywhere = pl.BlockSpec(memory_space=pltpu.VMEM), pl.BlockSpec(memory_space=pl.ANY)
    dma = pltpu.SemaphoreType.DMA
    return pl.pallas_call(
        functools.partial(
            body, n, rows, depth, parts, kept, page, per_owner, slot_most, pool_dev
        ),
        out_shape=jax.ShapeDtypeStruct((per_owner, seg, QPK * HD), bf16),
        in_specs=[
            anywhere, anywhere, vmem, vmem, pl.BlockSpec(memory_space=pltpu.SMEM), anywhere,
        ],
        out_specs=anywhere,
        scratch_shapes=[
            pltpu.VMEM((parts, rows, depth // parts), bf16),
            pltpu.VMEM((chunks, parts, depth // parts, CHUNK), bf16),
            pltpu.VMEM((chunks, 8, CHUNK), f32),
            pltpu.VMEM((rows, CHUNK), f32),
            pltpu.VMEM((rows, CHUNK), bf16),
            pltpu.VMEM((sessions * slot_most // CHUNK, CHUNK, rows), bf16),
            pltpu.VMEM((units, sessions, slot_most, UNIT), bf16),
            pltpu.VMEM((units, per_owner, seg, UNIT), bf16),
            pltpu.VMEM((n, page, pair), bf16),
            pltpu.VMEM((n, page, pair), bf16),
            pltpu.VMEM((pool_dev, page, pair), bf16),
            pltpu.VMEM((per_owner, hist + seg, HD), bf16),
            pltpu.VMEM((per_owner, hist + seg, 2 * HD), bf16),
            pltpu.VMEM((per_owner, seg, seg), f32),
            pltpu.VMEM((per_owner, seg, HD), f32),
            pltpu.VMEM((QPK, per_owner, seg, HD), bf16),
            dma((parts,)),
            dma((chunks, parts)),
            dma(()),
            dma(()),
            dma(()),
            dma((units,)),
            dma((units,)),
            dma((QPK,)),
        ],
        compiler_params=pltpu.CompilerParams(
            collective_id=0, has_side_effects=True, vmem_limit_bytes=62 * 2**20
        ),
        name="routed_attention",
    )(
        hidden,
        w_qkv[:, 0, :],
        b_qkv,
        routes.reshape(n, rows),
        jnp.transpose(page_lists, (1, 2, 0)),
        pool[:, 0],
    )


def solution(mesh):
    in_specs = (
        P("sess", None),
        P(),
        P(None, "tp", None),
        P("tp", None),
        P("sess", "tp", None, None),
        P(),
    )
    return jax.shard_map(
        on_device, mesh=mesh, in_specs=in_specs, out_specs=P("sess", None, "tp"), check_vma=False
    )
```

```python
import functools
import math

import jax
import jax.numpy as jnp
from jax import lax
from jax.experimental import pallas as pl
from jax.experimental.pallas import tpu as pltpu
from jax.sharding import PartitionSpec as P

HD = 128
QPK = 8
UNIT = 128
CHUNK = 256
MESH = pl.DeviceIdType.MESH
NT = (((1,), (1,)), ((), ()))


def body(
    n, rows, depth, parts, kept, page, per_owner, slot_most, pool_dev,
    hidden_hbm, w_hbm, bias_ref, routes_ref, lists_ref, pool_hbm, out_ref,
    hid, wv, biasv, acc, projv, place, send, recv, psend, precv, poolv,
    keys, vals, mask, alive, blocks,
    hid_sem, w_sem, pool_sem, ps_sem, pr_sem, send_sem, recv_sem,
):
    f32, bf16, i32 = jnp.float32, jnp.bfloat16, jnp.int32
    me = lax.axis_index("sess")
    head = lax.axis_index("tp")
    sessions = n * per_owner
    seg = n * slot_most
    hist = kept * page
    slots = sessions * slot_most
    chunks = (QPK + 2) * HD // CHUNK
    block = depth // parts

    planes = n // 8
    mine_x, mine_z, mine_c = lax.div(me, 8), lax.rem(lax.div(me, 2), 4), lax.rem(me, 2)

    def peer(k):
        at_x = lax.rem(mine_x + lax.div(k, 8), planes)
        at_z = lax.rem(mine_z + lax.rem(lax.div(k, 2), 4), 4)
        return (at_x * 4 + at_z) * 2 + lax.rem(mine_c + lax.rem(k, 2), 2)

    barrier = pltpu.get_barrier_semaphore()

    def pool_copy():
        return pltpu.make_async_copy(pool_hbm, poolv, pool_sem)

    pool_copy().start()

    def greet(k, carry):
        pl.semaphore_signal(
            barrier, inc=1, device_id={"sess": peer(k)}, device_id_type=MESH
        )
        return carry

    lax.fori_loop(1, n, greet, 0)

    def hid_copy(k):
        return pltpu.make_async_copy(
            hidden_hbm.at[:, pl.ds(k * block, block)], hid.at[k], hid_sem.at[k]
        )

    def w_copy(c, k):
        first = lax.rem(c + chunks - 1, chunks) * CHUNK
        return pltpu.make_async_copy(
            w_hbm.at[pl.ds(pl.multiple_of(k * block, block), block),
                     pl.ds(pl.multiple_of(first, CHUNK), CHUNK)],
            wv.at[lax.rem(c, 2), k],
            w_sem.at[lax.rem(c, 2), k],
        )

    pool_copy().wait()
    for k in range(parts):
        hid_copy(k).start()
        w_copy(jnp.int32(0), k).start()

    pl.semaphore_wait(barrier, n - 1)

    def page_copy(k):
        to = peer(k)
        return pltpu.make_async_remote_copy(
            src_ref=psend.at[to], dst_ref=precv.at[me], send_sem=ps_sem, recv_sem=pr_sem,
            device_id={"sess": to}, device_id_type=MESH,
        )

    def pick(k, carry):
        o = peer(k)
        chosen = jnp.int32(0)
        for l in range(per_owner):
            for i in range(kept):
                slot = lists_ref[head, i, o * per_owner + l] - me * pool_dev
                chosen += jnp.where((slot >= 0) & (slot < pool_dev), slot, 0)
        psend[o] = poolv[chosen]

        @pl.when(k > 1)
        def _():
            page_copy(k - 1).start()

        return carry

    lax.fori_loop(1, n, pick, 0)
    pick(0, 0)
    page_copy(n - 1).start()
    precv[me] = psend[me]

    destination = routes_ref[:, pl.ds(pl.multiple_of(me * rows, rows), rows)]
    onehot = (lax.broadcasted_iota(i32, (sessions, rows), 0) == destination).astype(f32)
    earlier = (
        lax.broadcasted_iota(i32, (rows, rows), 0) < lax.broadcasted_iota(i32, (rows, rows), 1)
    ).astype(bf16)
    before = jnp.dot(onehot.astype(bf16), earlier, preferred_element_type=f32)
    ranking = jnp.sum(onehot * before, axis=0, keepdims=True)
    target = destination.astype(f32) * float(slot_most) + ranking
    steps = slots // CHUNK

    def fill(m, carry):
        ids = lax.broadcasted_iota(i32, (CHUNK, rows), 0) + m * CHUNK
        place[m] = (ids.astype(f32) == target).astype(bf16)
        return carry

    lax.fori_loop(0, steps, fill, 0)

    for c in range(chunks):
        first = ((c + chunks - 1) % chunks) * CHUNK
        biasv[c] = jnp.broadcast_to(bias_ref[0:1, first : first + CHUNK], (8, CHUNK))

    def row_copy(u, k):
        to = peer(k)
        return pltpu.make_async_remote_copy(
            src_ref=send.at[u, pl.ds(to * per_owner, per_owner)],
            dst_ref=recv.at[u, :, pl.ds(pl.multiple_of(me * slot_most, slot_most), slot_most)],
            send_sem=send_sem.at[u], recv_sem=recv_sem.at[u],
            device_id={"sess": to}, device_id_type=MESH,
        )

    def project(c, carry):
        acc[...] = jnp.zeros_like(acc)

        def multiply(k, inner):
            @pl.when(c == 0)
            def _():
                hid_copy(k).wait()

            w_copy(c, k).wait()

            @pl.when(c < chunks - 1)
            def _():
                w_copy(c + 1, k).start()

            acc[...] += jnp.dot(hid[k], wv[lax.rem(c, 2), k], preferred_element_type=f32)
            return inner

        lax.fori_loop(0, parts, multiply, 0)
        projv[...] = (acc[...] + biasv[c][0:1, :]).astype(bf16)

        def put(m, inner):
            placed = jnp.dot(place[m], projv[...], preferred_element_type=f32).astype(bf16)
            group = CHUNK // slot_most
            at = pl.ds(m * group, group)
            send[2 * c, at] = placed[:, :UNIT].reshape(group, slot_most, UNIT)
            send[2 * c + 1, at] = placed[:, UNIT:].reshape(group, slot_most, UNIT)
            return inner

        lax.fori_loop(0, steps, put, 0)

        def ship(k, inner):
            row_copy(2 * c, k).start()
            row_copy(2 * c + 1, k).start()
            return inner

        lax.fori_loop(1, n, ship, 0)
        own = pl.ds(pl.multiple_of(me * slot_most, slot_most), slot_most)
        for u in range(2):
            recv[2 * c + u, :, own, :] = send[2 * c + u, pl.ds(me * per_owner, per_owner)]
        return carry

    lax.fori_loop(0, chunks, project, 0)

    def arrived(u):
        part = recv.at[u, :, pl.ds(0, seg - slot_most)]
        pltpu.make_async_copy(part, part, recv_sem.at[u]).wait()

    for b in range(n):
        blocks[b : b + 1, :] = routes_ref[:, b * rows : (b + 1) * rows]
    for l in range(per_owner):
        same = (blocks[...] == me * per_owner + l).astype(f32)
        count_col = jnp.sum(same, axis=1, keepdims=True)
        count_row = lax.dot_general(
            jnp.ones((8, rows), bf16), same.astype(bf16), NT, preferred_element_type=f32
        )
        spread = (
            lax.broadcasted_iota(i32, (n, seg), 1) // slot_most
            == lax.broadcasted_iota(i32, (n, seg), 0)
        ).astype(bf16)
        spread_t = (
            lax.broadcasted_iota(i32, (seg, n), 0) // slot_most
            == lax.broadcasted_iota(i32, (seg, n), 1)
        ).astype(bf16)
        row_counts = jnp.dot(count_row.astype(bf16), spread, preferred_element_type=f32)
        col_counts = jnp.dot(
            spread_t, jnp.broadcast_to(count_col, (n, HD)).astype(bf16),
            preferred_element_type=f32,
        )
        row_off = (lax.broadcasted_iota(i32, (8, seg), 1) % slot_most).astype(f32)
        col_off = (lax.broadcasted_iota(i32, (seg, HD), 0) % slot_most).astype(f32)
        alive[l] = (col_off < col_counts).astype(f32)
        live_row = jnp.where(row_off < row_counts, 0.0, -1e30)[0:1, :]
        mask[l] = jnp.where(
            lax.broadcasted_iota(i32, (seg, seg), 1) <= lax.broadcasted_iota(i32, (seg, seg), 0),
            live_row, -1e30,
        )
        vals[l, :, HD:] = jnp.ones((hist + seg, HD), bf16)

    part = precv.at[pl.ds(0, n - 1)]
    pltpu.make_async_copy(part, part, pr_sem).wait()
    for l in range(per_owner):
        for k in range(kept):
            source = lists_ref[head, k, me * per_owner + l] // pool_dev
            got = precv[source]
            keys[l, k * page : (k + 1) * page, :] = got[:, :HD]
            vals[l, k * page : (k + 1) * page, :HD] = got[:, HD:]
    arrived(0)
    arrived(1)
    for l in range(per_owner):
        keys[l, hist:, :] = recv[0, l]
        vals[l, hist:, :HD] = recv[1, l]

    tile = min(seg, 256)
    factor = math.log2(math.e) / math.sqrt(HD)

    def attend(h, carry):
        arrived(2 + h)
        for l in range(per_owner):
            for start in range(0, seg, tile):
                upto = start + tile
                query = recv[2 + h, l, start:upto, :]
                past = lax.dot_general(query, keys[l, :hist, :], NT, preferred_element_type=f32)
                turn = lax.dot_general(
                    query, keys[l, hist : hist + upto, :], NT, preferred_element_type=f32
                )
                turn = turn + mask[l, start:upto, :upto]
                top = jnp.maximum(
                    jnp.max(past, axis=1, keepdims=True), jnp.max(turn, axis=1, keepdims=True)
                )
                past = jnp.exp2((past - top) * factor).astype(bf16)
                turn = jnp.exp2((turn - top) * factor).astype(bf16)
                total = jnp.dot(past, vals[l, :hist, :], preferred_element_type=f32)
                total += jnp.dot(turn, vals[l, hist : hist + upto, :], preferred_element_type=f32)
                mixed = total[:, :HD] / total[:, HD:]
                mixed = jnp.where(alive[l, start:upto, :] > 0.0, mixed, 0.0)
                out_ref[l, start:upto, pl.ds(pl.multiple_of(h * HD, HD), HD)] = mixed.astype(bf16)
        return carry

    lax.fori_loop(0, QPK, attend, 0)

    part = psend.at[pl.ds(0, n - 1)]
    pltpu.make_async_copy(part, part, ps_sem).wait()

    def sent(u, carry):
        part = send.at[u, pl.ds(0, sessions - per_owner)]
        pltpu.make_async_copy(part, part, send_sem.at[u]).wait()
        return carry

    lax.fori_loop(0, 2 * chunks, sent, 0)


def on_device(hidden, routes, w_qkv, b_qkv, pool, page_lists):
    n = lax.axis_size("sess")
    rows, depth = hidden.shape
    sessions, _, kept = page_lists.shape
    per_owner = sessions // n
    slot_most = 2 * rows // sessions
    seg = n * slot_most
    pool_dev, _, page, pair = pool.shape
    hist = kept * page
    columns = (QPK + 2) * HD
    chunks = columns // CHUNK
    units = columns // UNIT
    parts = 8
    f32, bf16 = jnp.float32, jnp.bfloat16
    vmem, anywhere = pl.BlockSpec(memory_space=pltpu.VMEM), pl.BlockSpec(memory_space=pl.ANY)
    dma = pltpu.SemaphoreType.DMA
    return pl.pallas_call(
        functools.partial(
            body, n, rows, depth, parts, kept, page, per_owner, slot_most, pool_dev
        ),
        out_shape=jax.ShapeDtypeStruct((per_owner, seg, QPK * HD), bf16),
        in_specs=[
            anywhere, anywhere, vmem, vmem, pl.BlockSpec(memory_space=pltpu.SMEM), anywhere,
        ],
        out_specs=vmem,
        scratch_shapes=[
            pltpu.VMEM((parts, rows, depth // parts), bf16),
            pltpu.VMEM((2, parts, depth // parts, CHUNK), bf16),
            pltpu.VMEM((chunks, 8, CHUNK), f32),
            pltpu.VMEM((rows, CHUNK), f32),
            pltpu.VMEM((rows, CHUNK), bf16),
            pltpu.VMEM((sessions * slot_most // CHUNK, CHUNK, rows), bf16),
            pltpu.VMEM((units, sessions, slot_most, UNIT), bf16),
            pltpu.VMEM((units, per_owner, seg, UNIT), bf16),
            pltpu.VMEM((n, page, pair), bf16),
            pltpu.VMEM((n, page, pair), bf16),
            pltpu.VMEM((pool_dev, page, pair), bf16),
            pltpu.VMEM((per_owner, hist + seg, HD), bf16),
            pltpu.VMEM((per_owner, hist + seg, 2 * HD), bf16),
            pltpu.VMEM((per_owner, seg, seg), f32),
            pltpu.VMEM((per_owner, seg, HD), f32),
            pltpu.VMEM((n, rows), jnp.int32),
            dma((parts,)),
            dma((2, parts)),
            dma(()),
            dma(()),
            dma(()),
            dma((units,)),
            dma((units,)),
        ],
        compiler_params=pltpu.CompilerParams(
            collective_id=0, has_side_effects=True, vmem_limit_bytes=48 * 2**20
        ),
        name="routed_attention",
    )(
        hidden,
        w_qkv[:, 0, :],
        b_qkv,
        routes.T,
        jnp.transpose(page_lists, (1, 2, 0)),
        pool[:, 0],
    )


def solution(mesh):
    in_specs = (
        P("sess", None),
        P(),
        P(None, "tp", None),
        P("tp", None),
        P("sess", "tp", None, None),
        P(),
    )
    return jax.shard_map(
        on_device, mesh=mesh, in_specs=in_specs, out_specs=P("sess", None, "tp"), check_vma=False
    )
```

```python
import functools
import math

import jax
import jax.numpy as jnp
from jax import lax
from jax.experimental import pallas as pl
from jax.experimental.pallas import tpu as pltpu
from jax.sharding import PartitionSpec as P

HD = 128
QPK = 8
CHUNK = 256
MESH = pl.DeviceIdType.MESH
NT = (((1,), (1,)), ((), ()))


def body(
    n, rows, depth, parts, kept, page, per_owner, slot_most, pool_dev,
    hidden_hbm, w_hbm, bias_hbm, routes_hbm, lists_hbm, pool_hbm, out_ref,
    hid, wv, biasv, acc, projv, place, send, recv, psend, precv, poolv,
    keys, vals, mask, alive, blocks, bias_ref, routes_ref, lists_ref,
    hid_sem, w_sem, small_sem, ps_sem, pr_sem, send_sem, recv_sem,
):
    f32, bf16, i32 = jnp.float32, jnp.bfloat16, jnp.int32
    me = lax.axis_index("sess")
    head = lax.axis_index("tp")
    sessions = n * per_owner
    seg = n * slot_most
    hist = kept * page
    slots = sessions * slot_most
    chunks = (QPK + 2) * HD // CHUNK
    block = depth // parts

    planes = n // 8
    mine_x, mine_z, mine_c = lax.div(me, 8), lax.rem(lax.div(me, 2), 4), lax.rem(me, 2)
    at_x = [lax.rem(mine_x + d, planes) * 8 for d in range(planes)]
    at_z = [lax.rem(mine_z + d, 4) * 2 for d in range(4)]
    at_c = [mine_c, 1 - mine_c]
    offsets = [(x, z, c) for x in range(planes) for z in range(4) for c in range(2)][1:]
    offsets.sort(key=lambda o: (o[2],o[0],o[1]), reverse=True)
    peers = [at_x[x] + at_z[z] + at_c[c] for x, z, c in offsets]

    barrier = pltpu.get_barrier_semaphore()

    small = [
        pltpu.make_async_copy(pool_hbm, poolv, small_sem.at[0]),
        pltpu.make_async_copy(lists_hbm.at[head], lists_ref, small_sem.at[1]),
        pltpu.make_async_copy(routes_hbm, routes_ref, small_sem.at[2]),
        pltpu.make_async_copy(bias_hbm, bias_ref, small_sem.at[3]),
    ]
    for copy in small:
        copy.start()

    for to in peers:
        pl.semaphore_signal(barrier, inc=1, device_id={"sess": to}, device_id_type=MESH)

    def hid_copy(k):
        return pltpu.make_async_copy(
            hidden_hbm.at[:, pl.ds(k * block, block)], hid.at[k], hid_sem.at[k]
        )

    def w_copy(c, k):
        first = lax.rem(c + chunks - 1, chunks) * CHUNK
        return pltpu.make_async_copy(
            w_hbm.at[pl.ds(pl.multiple_of(k * block, block), block),
                     pl.ds(pl.multiple_of(first, CHUNK), CHUNK)],
            wv.at[lax.rem(c, 2), k],
            w_sem.at[lax.rem(c, 2), k],
        )

    for copy in small:
        copy.wait()
    for k in range(parts):
        hid_copy(k).start()
        w_copy(jnp.int32(0), k).start()

    pl.semaphore_wait(barrier, n - 1)

    def page_copy(to):
        return pltpu.make_async_remote_copy(
            src_ref=psend.at[to], dst_ref=precv.at[me], send_sem=ps_sem, recv_sem=pr_sem,
            device_id={"sess": to}, device_id_type=MESH,
        )

    picked = None
    for o in peers + [me]:
        chosen = jnp.int32(0)
        for l in range(per_owner):
            for i in range(kept):
                slot = lists_ref[i, o * per_owner + l] - me * pool_dev
                chosen += jnp.where((slot >= 0) & (slot < pool_dev), slot, 0)
        psend[o] = poolv[chosen]
        if picked is not None:
            page_copy(picked).start()
        picked = o
    precv[me] = psend[me]

    destination = routes_ref[:, pl.ds(pl.multiple_of(me * rows, rows), rows)]
    onehot = (lax.broadcasted_iota(i32, (sessions, rows), 0) == destination).astype(f32)
    earlier = (
        lax.broadcasted_iota(i32, (rows, rows), 0) < lax.broadcasted_iota(i32, (rows, rows), 1)
    ).astype(bf16)
    before = jnp.dot(onehot.astype(bf16), earlier, preferred_element_type=f32)
    ranking = jnp.sum(onehot * before, axis=0, keepdims=True)
    target = destination.astype(f32) * float(slot_most) + ranking
    steps = slots // CHUNK

    def fill(m, carry):
        ids = lax.broadcasted_iota(i32, (CHUNK, rows), 0) + m * CHUNK
        place[m] = (ids.astype(f32) == target).astype(bf16)
        return carry

    lax.fori_loop(0, steps, fill, 0)

    for c in range(chunks):
        first = ((c + chunks - 1) % chunks) * CHUNK
        biasv[c] = jnp.broadcast_to(bias_ref[0:1, first : first + CHUNK], (8, CHUNK))

    def row_copy(c, to, columns, sem):
        here = pl.ds(pl.multiple_of(me * slot_most, slot_most), slot_most)
        return pltpu.make_async_remote_copy(
            src_ref=send.at[c, pl.ds(to * per_owner, per_owner), :, columns],
            dst_ref=recv.at[c, :, here, columns],
            send_sem=send_sem.at[sem], recv_sem=recv_sem.at[sem],
            device_id={"sess": to}, device_id_type=MESH,
        )

    def project(c, carry):
        acc[...] = jnp.zeros_like(acc)

        def multiply(k, inner):
            @pl.when(c == 0)
            def _():
                hid_copy(k).wait()

            w_copy(c, k).wait()

            @pl.when(c < chunks - 1)
            def _():
                w_copy(c + 1, k).start()

            acc[...] += jnp.dot(hid[k], wv[lax.rem(c, 2), k], preferred_element_type=f32)
            return inner

        lax.fori_loop(0, parts, multiply, 0)
        projv[...] = (acc[...] + biasv[c][0:1, :]).astype(bf16)

        def put(m, inner):
            placed = jnp.dot(place[m], projv[...], preferred_element_type=f32).astype(bf16)
            group = CHUNK // slot_most
            at = pl.ds(m * group, group)
            send[c, at] = placed.reshape(group, slot_most, CHUNK)
            return inner

        lax.fori_loop(0, steps, put, 0)

        @pl.when(c < chunks - 1)
        def _():
            for to in peers:
                row_copy(c, to, pl.ds(0, CHUNK), c).start()

        @pl.when(c == chunks - 1)
        def _():
            for half in range(2):
                for to in peers:
                    row_copy(c, to, pl.ds(half * HD, HD), chunks - 1 + half).start()

        own = pl.ds(pl.multiple_of(me * slot_most, slot_most), slot_most)
        recv[c, :, own, :] = send[c, pl.ds(me * per_owner, per_owner)]
        return carry

    lax.fori_loop(0, chunks, project, 0)

    def arrived(u):
        part = recv.at[u, :, pl.ds(0, seg - slot_most)]
        pltpu.make_async_copy(part, part, recv_sem.at[u]).wait()

    for b in range(n):
        blocks[b : b + 1, :] = routes_ref[:, b * rows : (b + 1) * rows]
    for l in range(per_owner):
        same = (blocks[...] == me * per_owner + l).astype(f32)
        count_col = jnp.sum(same, axis=1, keepdims=True)
        count_row = lax.dot_general(
            jnp.ones((8, rows), bf16), same.astype(bf16), NT, preferred_element_type=f32
        )
        spread = (
            lax.broadcasted_iota(i32, (n, seg), 1) // slot_most
            == lax.broadcasted_iota(i32, (n, seg), 0)
        ).astype(bf16)
        spread_t = (
            lax.broadcasted_iota(i32, (seg, n), 0) // slot_most
            == lax.broadcasted_iota(i32, (seg, n), 1)
        ).astype(bf16)
        row_counts = jnp.dot(count_row.astype(bf16), spread, preferred_element_type=f32)
        col_counts = jnp.dot(
            spread_t, jnp.broadcast_to(count_col, (n, HD)).astype(bf16),
            preferred_element_type=f32,
        )
        row_off = (lax.broadcasted_iota(i32, (8, seg), 1) % slot_most).astype(f32)
        col_off = (lax.broadcasted_iota(i32, (seg, HD), 0) % slot_most).astype(f32)
        alive[l] = (col_off < col_counts).astype(f32)
        live_row = jnp.where(row_off < row_counts, 0.0, -1e30)[0:1, :]
        mask[l] = jnp.where(
            lax.broadcasted_iota(i32, (seg, seg), 1) <= lax.broadcasted_iota(i32, (seg, seg), 0),
            live_row, -1e30,
        )
        vals[l, :, HD:] = jnp.ones((hist + seg, HD), bf16)

    part = precv.at[pl.ds(0, n - 1)]
    pltpu.make_async_copy(part, part, pr_sem).wait()
    for l in range(per_owner):
        for k in range(kept):
            source = lists_ref[k, me * per_owner + l] // pool_dev
            got = precv[source]
            keys[l, k * page : (k + 1) * page, :] = got[:, :HD]
            vals[l, k * page : (k + 1) * page, :HD] = got[:, HD:]
    arrived(0)
    for l in range(per_owner):
        keys[l, hist:, :] = recv[0, l, :, :HD]
        vals[l, hist:, :HD] = recv[0, l, :, HD:]

    tile = min(seg, 256)
    factor = math.log2(math.e) / math.sqrt(HD)

    def attend(h, carry):
        @pl.when((lax.rem(h, 2) == 0) & (h < QPK - 2))
        def _():
            arrived(1 + lax.div(h, 2))

        @pl.when(h >= QPK - 2)
        def _():
            part = recv.at[chunks - 1, :, pl.ds(0, seg - slot_most), pl.ds(0, HD)]
            pltpu.make_async_copy(part, part, recv_sem.at[chunks - 1 + h - (QPK - 2)]).wait()

        half = pl.ds(pl.multiple_of(lax.rem(h, 2) * HD, HD), HD)
        for l in range(per_owner):
            for start in range(0, seg, tile):
                upto = start + tile
                query = recv[1 + lax.div(h, 2), l, start:upto, half]
                past = lax.dot_general(query, keys[l, :hist, :], NT, preferred_element_type=f32)
                turn = lax.dot_general(
                    query, keys[l, hist : hist + upto, :], NT, preferred_element_type=f32
                )
                turn = turn + mask[l, start:upto, :upto]
                top = jnp.maximum(
                    jnp.max(past, axis=1, keepdims=True), jnp.max(turn, axis=1, keepdims=True)
                )
                past = jnp.exp2((past - top) * factor).astype(bf16)
                turn = jnp.exp2((turn - top) * factor).astype(bf16)
                total = jnp.dot(past, vals[l, :hist, :], preferred_element_type=f32)
                total += jnp.dot(turn, vals[l, hist : hist + upto, :], preferred_element_type=f32)
                mixed = total[:, :HD] / total[:, HD:]
                mixed = jnp.where(alive[l, start:upto, :] > 0.0, mixed, 0.0)
                out_ref[l, start:upto, pl.ds(pl.multiple_of(h * HD, HD), HD)] = mixed.astype(bf16)
        return carry

    lax.fori_loop(0, QPK, attend, 0)

    part = psend.at[pl.ds(0, n - 1)]
    pltpu.make_async_copy(part, part, ps_sem).wait()

    def sent(u, carry):
        part = send.at[u, pl.ds(0, sessions - per_owner)]
        pltpu.make_async_copy(part, part, send_sem.at[u]).wait()
        return carry

    lax.fori_loop(0, chunks - 1, sent, 0)
    part = send.at[chunks - 1, pl.ds(0, sessions - per_owner), :, pl.ds(0, HD)]
    for half in range(2):
        pltpu.make_async_copy(part, part, send_sem.at[chunks - 1 + half]).wait()


def on_device(hidden, routes, w_qkv, b_qkv, pool, page_lists):
    n = lax.axis_size("sess")
    rows, depth = hidden.shape
    sessions, _, kept = page_lists.shape
    per_owner = sessions // n
    slot_most = 2 * rows // sessions
    seg = n * slot_most
    pool_dev, _, page, pair = pool.shape
    hist = kept * page
    columns = (QPK + 2) * HD
    chunks = columns // CHUNK
    parts = 8
    f32, bf16 = jnp.float32, jnp.bfloat16
    vmem, hbm = pl.BlockSpec(memory_space=pltpu.VMEM), pl.BlockSpec(memory_space=pltpu.HBM)
    dma = pltpu.SemaphoreType.DMA
    return pl.pallas_call(
        functools.partial(
            body, n, rows, depth, parts, kept, page, per_owner, slot_most, pool_dev
        ),
        out_shape=jax.ShapeDtypeStruct((per_owner, seg, QPK * HD), bf16),
        in_specs=[hbm] * 6,
        out_specs=vmem,
        scratch_shapes=[
            pltpu.VMEM((parts, rows, depth // parts), bf16),
            pltpu.VMEM((2, parts, depth // parts, CHUNK), bf16),
            pltpu.VMEM((chunks, 8, CHUNK), f32),
            pltpu.VMEM((rows, CHUNK), f32),
            pltpu.VMEM((rows, CHUNK), bf16),
            pltpu.VMEM((sessions * slot_most // CHUNK, CHUNK, rows), bf16),
            pltpu.VMEM((chunks, sessions, slot_most, CHUNK), bf16),
            pltpu.VMEM((chunks, per_owner, seg, CHUNK), bf16),
            pltpu.VMEM((n, page, pair), bf16),
            pltpu.VMEM((n, page, pair), bf16),
            pltpu.VMEM((pool_dev, page, pair), bf16),
            pltpu.VMEM((per_owner, hist + seg, HD), bf16),
            pltpu.VMEM((per_owner, hist + seg, 2 * HD), bf16),
            pltpu.VMEM((per_owner, seg, seg), f32),
            pltpu.VMEM((per_owner, seg, HD), f32),
            pltpu.VMEM((n, rows), jnp.int32),
            pltpu.VMEM((1, columns), f32),
            pltpu.VMEM((1, n * rows), jnp.int32),
            pltpu.SMEM((kept, sessions), jnp.int32),
            dma((parts,)),
            dma((2, parts)),
            dma((4,)),
            dma(()),
            dma(()),
            dma((chunks + 1,)),
            dma((chunks + 1,)),
        ],
        compiler_params=pltpu.CompilerParams(
            collective_id=0, has_side_effects=True, vmem_limit_bytes=48 * 2**20
        ),
        name="routed_attention",
    )(
        *[
            pltpu.with_memory_space_constraint(array, pltpu.HBM)
            for array in (
                hidden,
                w_qkv[:, 0, :],
                b_qkv,
                routes.T,
                jnp.transpose(page_lists, (1, 2, 0)),
                pool[:, 0],
            )
        ]
    )


def solution(mesh):
    in_specs = (
        P("sess", None),
        P(),
        P(None, "tp", None),
        P("tp", None),
        P("sess", "tp", None, None),
        P(),
    )
    return jax.shard_map(
        on_device, mesh=mesh, in_specs=in_specs, out_specs=P("sess", None, "tp"), check_vma=False
    )
```

```python
import functools
import math

import jax
import jax.numpy as jnp
from jax import lax
from jax.experimental import pallas as pl
from jax.experimental.pallas import tpu as pltpu
from jax.sharding import PartitionSpec as P

HD = 128
QPK = 8
CHUNK = 256
MESH = pl.DeviceIdType.MESH
NT = (((1,), (1,)), ((), ()))


def body(
    n, rows, depth, parts, kept, page, per_owner, slot_most, pool_dev,
    hidden_hbm, w_hbm, bias_hbm, routes_hbm, lists_hbm, pool_hbm, out_ref,
    hid, wv, biasv, acc, projv, place, send, recv, psend, precv, poolv,
    keys, vals, mask, alive, blocks, bias_ref, routes_ref, lists_ref,
    hid_sem, w_sem, small_sem, ps_sem, pr_sem, send_sem, recv_sem,
):
    f32, bf16, i32 = jnp.float32, jnp.bfloat16, jnp.int32
    me = lax.axis_index("sess")
    head = lax.axis_index("tp")
    sessions = n * per_owner
    seg = n * slot_most
    hist = kept * page
    slots = sessions * slot_most
    chunks = (QPK + 2) * HD // CHUNK
    block = depth // parts

    planes = n // 8
    mine_x, mine_z, mine_c = lax.div(me, 8), lax.rem(lax.div(me, 2), 4), lax.rem(me, 2)
    at_x = [lax.rem(mine_x + d, planes) * 8 for d in range(planes)]
    at_z = [lax.rem(mine_z + d, 4) * 2 for d in range(4)]
    at_c = [mine_c, 1 - mine_c]
    offsets = [(x, z, c) for x in range(planes) for z in range(4) for c in range(2)][1:]
    offsets.sort(key=lambda o: (o[2],o[0],o[1]), reverse=True)
    peers = [at_x[x] + at_z[z] + at_c[c] for x, z, c in offsets]

    barrier = pltpu.get_barrier_semaphore()

    small = [
        pltpu.make_async_copy(pool_hbm, poolv, small_sem.at[0]),
        pltpu.make_async_copy(lists_hbm.at[head], lists_ref, small_sem.at[1]),
        pltpu.make_async_copy(routes_hbm, routes_ref, small_sem.at[2]),
        pltpu.make_async_copy(bias_hbm, bias_ref, small_sem.at[3]),
    ]

    for to in peers:
        pl.semaphore_signal(barrier, inc=1, device_id={"sess": to}, device_id_type=MESH)

    for copy in small:
        copy.start()

    def hid_copy(k):
        return pltpu.make_async_copy(
            hidden_hbm.at[:, pl.ds(k * block, block)], hid.at[k], hid_sem.at[k]
        )

    def w_copy(c, k):
        first = lax.rem(c + chunks - 1, chunks) * CHUNK
        return pltpu.make_async_copy(
            w_hbm.at[pl.ds(pl.multiple_of(k * block, block), block),
                     pl.ds(pl.multiple_of(first, CHUNK), CHUNK)],
            wv.at[lax.rem(c, 2), k],
            w_sem.at[lax.rem(c, 2), k],
        )

    for copy in small:
        copy.wait()
    for k in range(parts):
        hid_copy(k).start()
        w_copy(jnp.int32(0), k).start()

    pl.semaphore_wait(barrier, n - 1)

    def page_copy(to):
        return pltpu.make_async_remote_copy(
            src_ref=psend.at[to], dst_ref=precv.at[me], send_sem=ps_sem, recv_sem=pr_sem,
            device_id={"sess": to}, device_id_type=MESH,
        )

    picked = None
    for o in peers + [me]:
        chosen = jnp.int32(0)
        for l in range(per_owner):
            for i in range(kept):
                slot = lists_ref[i, o * per_owner + l] - me * pool_dev
                chosen += jnp.where((slot >= 0) & (slot < pool_dev), slot, 0)
        psend[o] = poolv[chosen]
        if picked is not None:
            page_copy(picked).start()
        picked = o
    precv[me] = psend[me]

    destination = routes_ref[:, pl.ds(pl.multiple_of(me * rows, rows), rows)]
    onehot = (lax.broadcasted_iota(i32, (sessions, rows), 0) == destination).astype(f32)
    earlier = (
        lax.broadcasted_iota(i32, (rows, rows), 0) < lax.broadcasted_iota(i32, (rows, rows), 1)
    ).astype(bf16)
    before = jnp.dot(onehot.astype(bf16), earlier, preferred_element_type=f32)
    ranking = jnp.sum(onehot * before, axis=0, keepdims=True)
    target = destination.astype(f32) * float(slot_most) + ranking
    steps = slots // CHUNK

    def fill(m, carry):
        ids = lax.broadcasted_iota(i32, (CHUNK, rows), 0) + m * CHUNK
        place[m] = (ids.astype(f32) == target).astype(bf16)
        return carry

    lax.fori_loop(0, steps, fill, 0)

    for c in range(chunks):
        first = ((c + chunks - 1) % chunks) * CHUNK
        biasv[c] = jnp.broadcast_to(bias_ref[0:1, first : first + CHUNK], (8, CHUNK))

    def row_copy(c, to, columns, sem):
        here = pl.ds(pl.multiple_of(me * slot_most, slot_most), slot_most)
        return pltpu.make_async_remote_copy(
            src_ref=send.at[c, pl.ds(to * per_owner, per_owner), :, columns],
            dst_ref=recv.at[c, :, here, columns],
            send_sem=send_sem.at[sem], recv_sem=recv_sem.at[sem],
            device_id={"sess": to}, device_id_type=MESH,
        )

    def project(c, carry):
        acc[...] = jnp.zeros_like(acc)

        def multiply(k, inner):
            @pl.when(c == 0)
            def _():
                hid_copy(k).wait()

            w_copy(c, k).wait()

            @pl.when(c < chunks - 1)
            def _():
                w_copy(c + 1, k).start()

            acc[...] += jnp.dot(hid[k], wv[lax.rem(c, 2), k], preferred_element_type=f32)
            return inner

        lax.fori_loop(0, parts, multiply, 0)
        projv[...] = (acc[...] + biasv[c][0:1, :]).astype(bf16)

        def put(m, inner):
            placed = jnp.dot(place[m], projv[...], preferred_element_type=f32).astype(bf16)
            group = CHUNK // slot_most
            at = pl.ds(m * group, group)
            send[c, at] = placed.reshape(group, slot_most, CHUNK)
            return inner

        lax.fori_loop(0, steps, put, 0)

        @pl.when(c < chunks - 1)
        def _():
            for to in peers:
                row_copy(c, to, pl.ds(0, CHUNK), c).start()

        @pl.when(c == chunks - 1)
        def _():
            for half in range(2):
                for to in peers:
                    row_copy(c, to, pl.ds(half * HD, HD), chunks - 1 + half).start()

        own = pl.ds(pl.multiple_of(me * slot_most, slot_most), slot_most)
        recv[c, :, own, :] = send[c, pl.ds(me * per_owner, per_owner)]
        return carry

    lax.fori_loop(0, chunks, project, 0)

    def arrived(u):
        part = recv.at[u, :, pl.ds(0, seg - slot_most)]
        pltpu.make_async_copy(part, part, recv_sem.at[u]).wait()

    for b in range(n):
        blocks[b : b + 1, :] = routes_ref[:, b * rows : (b + 1) * rows]
    for l in range(per_owner):
        same = (blocks[...] == me * per_owner + l).astype(f32)
        count_col = jnp.sum(same, axis=1, keepdims=True)
        count_row = lax.dot_general(
            jnp.ones((8, rows), bf16), same.astype(bf16), NT, preferred_element_type=f32
        )
        spread = (
            lax.broadcasted_iota(i32, (n, seg), 1) // slot_most
            == lax.broadcasted_iota(i32, (n, seg), 0)
        ).astype(bf16)
        spread_t = (
            lax.broadcasted_iota(i32, (seg, n), 0) // slot_most
            == lax.broadcasted_iota(i32, (seg, n), 1)
        ).astype(bf16)
        row_counts = jnp.dot(count_row.astype(bf16), spread, preferred_element_type=f32)
        col_counts = jnp.dot(
            spread_t, jnp.broadcast_to(count_col, (n, HD)).astype(bf16),
            preferred_element_type=f32,
        )
        row_off = (lax.broadcasted_iota(i32, (8, seg), 1) % slot_most).astype(f32)
        col_off = (lax.broadcasted_iota(i32, (seg, HD), 0) % slot_most).astype(f32)
        alive[l] = (col_off < col_counts).astype(f32)
        live_row = jnp.where(row_off < row_counts, 0.0, -1e30)[0:1, :]
        mask[l] = jnp.where(
            lax.broadcasted_iota(i32, (seg, seg), 1) <= lax.broadcasted_iota(i32, (seg, seg), 0),
            live_row, -1e30,
        )
        vals[l, :, HD:] = jnp.ones((hist + seg, HD), bf16)

    part = precv.at[pl.ds(0, n - 1)]
    pltpu.make_async_copy(part, part, pr_sem).wait()
    for l in range(per_owner):
        for k in range(kept):
            source = lists_ref[k, me * per_owner + l] // pool_dev
            got = precv[source]
            keys[l, k * page : (k + 1) * page, :] = got[:, :HD]
            vals[l, k * page : (k + 1) * page, :HD] = got[:, HD:]
    arrived(0)
    for l in range(per_owner):
        keys[l, hist:, :] = recv[0, l, :, :HD]
        vals[l, hist:, :HD] = recv[0, l, :, HD:]

    tile = min(seg, 256)
    factor = math.log2(math.e) / math.sqrt(HD)

    def attend(h, carry):
        @pl.when((lax.rem(h, 2) == 0) & (h < QPK - 2))
        def _():
            arrived(1 + lax.div(h, 2))

        @pl.when(h >= QPK - 2)
        def _():
            part = recv.at[chunks - 1, :, pl.ds(0, seg - slot_most), pl.ds(0, HD)]
            pltpu.make_async_copy(part, part, recv_sem.at[chunks - 1 + h - (QPK - 2)]).wait()

        half = pl.ds(pl.multiple_of(lax.rem(h, 2) * HD, HD), HD)
        for l in range(per_owner):
            for start in range(0, seg, tile):
                upto = start + tile
                query = recv[1 + lax.div(h, 2), l, start:upto, half]
                past = lax.dot_general(query, keys[l, :hist, :], NT, preferred_element_type=f32)
                turn = lax.dot_general(
                    query, keys[l, hist : hist + upto, :], NT, preferred_element_type=f32
                )
                turn = turn + mask[l, start:upto, :upto]
                top = jnp.maximum(
                    jnp.max(past, axis=1, keepdims=True), jnp.max(turn, axis=1, keepdims=True)
                )
                past = jnp.exp2((past - top) * factor).astype(bf16)
                turn = jnp.exp2((turn - top) * factor).astype(bf16)
                total = jnp.dot(past, vals[l, :hist, :], preferred_element_type=f32)
                total += jnp.dot(turn, vals[l, hist : hist + upto, :], preferred_element_type=f32)
                mixed = total[:, :HD] / total[:, HD:]
                mixed = jnp.where(alive[l, start:upto, :] > 0.0, mixed, 0.0)
                out_ref[l, start:upto, pl.ds(pl.multiple_of(h * HD, HD), HD)] = mixed.astype(bf16)
        return carry

    lax.fori_loop(0, QPK, attend, 0)

    part = psend.at[pl.ds(0, n - 1)]
    pltpu.make_async_copy(part, part, ps_sem).wait()

    def sent(u, carry):
        part = send.at[u, pl.ds(0, sessions - per_owner)]
        pltpu.make_async_copy(part, part, send_sem.at[u]).wait()
        return carry

    lax.fori_loop(0, chunks - 1, sent, 0)
    part = send.at[chunks - 1, pl.ds(0, sessions - per_owner), :, pl.ds(0, HD)]
    for half in range(2):
        pltpu.make_async_copy(part, part, send_sem.at[chunks - 1 + half]).wait()


def on_device(hidden, routes, w_qkv, b_qkv, pool, page_lists):
    n = lax.axis_size("sess")
    rows, depth = hidden.shape
    sessions, _, kept = page_lists.shape
    per_owner = sessions // n
    slot_most = 2 * rows // sessions
    seg = n * slot_most
    pool_dev, _, page, pair = pool.shape
    hist = kept * page
    columns = (QPK + 2) * HD
    chunks = columns // CHUNK
    parts = 8
    f32, bf16 = jnp.float32, jnp.bfloat16
    vmem, hbm = pl.BlockSpec(memory_space=pltpu.VMEM), pl.BlockSpec(memory_space=pltpu.HBM)
    dma = pltpu.SemaphoreType.DMA
    return pl.pallas_call(
        functools.partial(
            body, n, rows, depth, parts, kept, page, per_owner, slot_most, pool_dev
        ),
        out_shape=jax.ShapeDtypeStruct((per_owner, seg, QPK * HD), bf16),
        in_specs=[hbm] * 6,
        out_specs=vmem,
        scratch_shapes=[
            pltpu.VMEM((parts, rows, depth // parts), bf16),
            pltpu.VMEM((2, parts, depth // parts, CHUNK), bf16),
            pltpu.VMEM((chunks, 8, CHUNK), f32),
            pltpu.VMEM((rows, CHUNK), f32),
            pltpu.VMEM((rows, CHUNK), bf16),
            pltpu.VMEM((sessions * slot_most // CHUNK, CHUNK, rows), bf16),
            pltpu.VMEM((chunks, sessions, slot_most, CHUNK), bf16),
            pltpu.VMEM((chunks, per_owner, seg, CHUNK), bf16),
            pltpu.VMEM((n, page, pair), bf16),
            pltpu.VMEM((n, page, pair), bf16),
            pltpu.VMEM((pool_dev, page, pair), bf16),
            pltpu.VMEM((per_owner, hist + seg, HD), bf16),
            pltpu.VMEM((per_owner, hist + seg, 2 * HD), bf16),
            pltpu.VMEM((per_owner, seg, seg), f32),
            pltpu.VMEM((per_owner, seg, HD), f32),
            pltpu.VMEM((n, rows), jnp.int32),
            pltpu.VMEM((1, columns), f32),
            pltpu.VMEM((1, n * rows), jnp.int32),
            pltpu.SMEM((kept, sessions), jnp.int32),
            dma((parts,)),
            dma((2, parts)),
            dma((4,)),
            dma(()),
            dma(()),
            dma((chunks + 1,)),
            dma((chunks + 1,)),
        ],
        compiler_params=pltpu.CompilerParams(
            collective_id=0, has_side_effects=True, vmem_limit_bytes=48 * 2**20
        ),
        name="routed_attention",
    )(
        *[
            pltpu.with_memory_space_constraint(array, pltpu.HBM)
            for array in (
                hidden,
                w_qkv[:, 0, :],
                b_qkv,
                routes.T,
                jnp.transpose(page_lists, (1, 2, 0)),
                pool[:, 0],
            )
        ]
    )


def solution(mesh):
    in_specs = (
        P("sess", None),
        P(),
        P(None, "tp", None),
        P("tp", None),
        P("sess", "tp", None, None),
        P(),
    )
    return jax.shard_map(
        on_device, mesh=mesh, in_specs=in_specs, out_specs=P("sess", None, "tp"), check_vma=False
    )
```
